256 devices in a mesh: pipe: 8 (over z), dp: 4 (over y), expert: 8 (over x, core).
Axes of the slice: x: 4, y: 4, z: 8, core: 2. Of those that a mesh axis runs over, the one named last changes fastest.
Arguments:
- tokens: bfloat16 [4096, 4096], P(('dp', 'expert'), 'pipe'), may hold values from -6 to 6
- routes: int32 [4096, 6], P(('dp', 'expert')), may hold values from 0 to 31, all different within a row; in each aligned block of 128 rows (0 to 127, 128 to 255, ...) at most 32 rows name the same one
- gates: float32 [4096, 6], P(('dp', 'expert')), may hold values from 0.1 to 0.5
- w_gate: bfloat16 [32, 4096, 1024], P(('dp', 'expert'), 'pipe'), may hold values from -0.09375 to 0.09375
- w_up: bfloat16 [32, 4096, 1024], P(('dp', 'expert'), 'pipe'), may hold values from -0.09375 to 0.09375
- w_down: bfloat16 [32, 1024, 4096], P(('dp', 'expert'), None, 'pipe'), may hold values from -0.1875 to 0.1875
- grad_out: bfloat16 [4096, 4096], P(('dp', 'expert'), 'pipe'), may hold values from -6 to 6
Outputs:
- mixed: bfloat16 [4096, 4096], P(('dp', 'expert'), 'pipe')
- grad_tokens: bfloat16 [4096, 4096], P(('dp', 'expert'), 'pipe')
- grad_gate: bfloat16 [32, 4096, 1024], P(('dp', 'expert'), 'pipe')
- grad_up: bfloat16 [32, 4096, 1024], P(('dp', 'expert'), 'pipe')
- grad_down: bfloat16 [32, 1024, 4096], P(('dp', 'expert'), None, 'pipe')
The draws below stay inside these ranges and needn't reach their ends.
Inputs may be any that keep to these rules, and one draw needn't show every extreme that they name: `routes`: each row names 6 different experts; in each aligned block of 128 rows no expert is named by more than 32 rows, a bound that some block reaches.
All inputs are finite; a program needn't handle non-finite values.
Results may differ from the reference program's by a relative error of at most 0.0065.
Values may be sent and summed in bfloat16 or wider, within the bound.
A program may use at most 128 MiB of HBM per device.

```python
import math
import jax
import jax.numpy as jnp
import numpy as np
from jax import lax

D = 4096
FF = 1024
EXPERTS = 32
TOP = 6
TOK_DEV = 128
CAP = 32
TOKENS = 4096


def levels(own_key, dims, pieces, smallest, top_value):
    def one(dim, parts):
        steps = jax.random.uniform(jax.random.fold_in(jax.random.fold_in(own_key, 6), dim), (parts,), jnp.float32, smallest / len(pieces), top_value / len(pieces))
        return jnp.repeat(jnp.exp(steps), dims[dim] // parts).reshape((-1,) + (1,) * (len(dims) - dim - 1))

    factor_of = one(*pieces[0])
    for cut in pieces[1:]:
        factor_of = factor_of * one(*cut)
    return factor_of


def deal_out(key, own, number, rows, number_of, top, reach, lean):
    ranking = jax.random.permutation(key, number_of)
    packed, common = load_shares(number_of, rows * top, reach, lean, True), load_shares(number_of, rows * top, reach, lean, False)
    places = jnp.arange(number_of)

    def named(tallies, rotation):
        used = int((tallies > 0).sum())
        fixed = max(1, used // 4)
        moved = fixed + (places - fixed + rotation * (used - fixed)) % max(1, number_of - fixed)
        return jnp.zeros((number_of,), jnp.int32).at[ranking[jnp.where(places < fixed, places, moved)]].set(jnp.asarray(tallies, jnp.int32))

    tallies = jnp.where(number % 4 == 0, named(packed, number // 4), named(common, number - number // 4 - 1))
    mixed = jax.random.permutation(jax.random.fold_in(own, 3), number_of)
    donor, taker = mixed[0:number_of // 2 * 2:2], mixed[1:number_of // 2 * 2:2]
    margin = jnp.minimum(tallies[donor] - 1, reach - tallies[taker]) // 2
    margin = jnp.where((donor == ranking[0]) | (taker == ranking[0]) | (tallies[taker] == 0), 0, jnp.maximum(margin, 0))
    moved = jax.random.randint(jax.random.fold_in(own, 4), (number_of // 2,), 0, 1 << 20) % (margin + 1)
    tallies = tallies.at[donor].add(-moved).at[taker].add(moved)
    members = jnp.searchsorted(jnp.cumsum(tallies), jnp.arange(rows * top), side="right").astype(jnp.int32)
    table = members.reshape(top, rows).T
    table = table[jax.random.permutation(jax.random.fold_in(own, 1), rows)]
    rotation = jax.random.randint(jax.random.fold_in(own, 2), (rows, 1), 0, top)
    return jnp.take_along_axis(table, (jnp.arange(top)[None, :] + rotation) % top, axis=1)


def load_shares(amount, total, bound, skew, full):
    portions = [(1 << 20) // math.isqrt(grade ** skew) + 1 for grade in range(1, amount + 1)]
    largest = bound if full else min(bound, max(-(-total // amount), total * portions[0] // sum(portions)))
    least = 1 if total - largest >= amount - 1 else 0
    counts, surplus = [largest] + [least] * (amount - 1), total - largest - least * (amount - 1)
    while surplus > 0:
        movable = [i for i in range(1, amount) if counts[i] < largest] or [i for i in range(1, amount) if counts[i] < bound]
        mass, left = sum([portions[i] for i in movable]), surplus
        for i in movable:
            extra = min(bound - counts[i], max(1, left * portions[i] // mass), surplus)
            counts[i] = counts[i] + extra
            surplus = surplus - extra
    return np.array(counts)


def normal_values(own_key, dims, deviation, reach, pieces=(), held_as=jnp.bfloat16):
    factor_of = levels(own_key, dims, pieces, -0.22, 0.18) if pieces else 1.0
    values = jax.random.normal(own_key, dims, jnp.float32) * deviation * factor_of
    return jnp.minimum(jnp.maximum(values, -reach), reach).astype(held_as)


def setup_inputs(seed: int = 0) -> dict:
    keys = jax.random.split(jax.random.key(seed), 8)
    tokens = normal_values(keys[0], (TOKENS, D), 1.0, 6.0, ((0, 32), (1, 8)))
    routes_keys = jax.random.split(jax.random.fold_in(keys[1], 1), TOKENS // TOK_DEV)
    routes_turns = jax.random.permutation(jax.random.fold_in(keys[1], 3), TOKENS // TOK_DEV)
    routes = jax.vmap(lambda own, number: deal_out(jax.random.fold_in(keys[1], 2), own, number, TOK_DEV, EXPERTS, TOP, CAP, 2))(routes_keys, routes_turns).reshape((TOKENS, TOP))
    gates = jnp.clip(0.1 + 0.4 * jax.random.uniform(keys[2], (TOKENS, TOP), jnp.float32) ** levels(keys[2], (TOKENS, TOP), ((0, 32),), -0.2, 0.2), 0.1, 0.5)
    w_gate = normal_values(keys[3], (EXPERTS, D, FF), D ** -0.5, 0.09375, ((0, 32), (1, 8)))
    w_up = normal_values(keys[4], (EXPERTS, D, FF), D ** -0.5, 0.09375, ((0, 32), (1, 8)))
    w_down = normal_values(keys[5], (EXPERTS, FF, D), FF ** -0.5, 0.1875, ((0, 32), (2, 8)))
    grad_out = normal_values(keys[6], (TOKENS, D), 1.0, 6.0, ((0, 32), (1, 8)))
    return {"tokens": tokens, "routes": routes, "gates": gates, "w_gate": w_gate, "w_up": w_up, "w_down": w_down, "grad_out": grad_out}


def reference(tokens, routes, gates, w_gate, w_up, w_down, grad_out):
    num_blocks = TOKENS // TOK_DEV
    per_block = TOK_DEV * TOP
    chosen = routes.reshape(num_blocks, per_block)
    gate_flat = gates.reshape(num_blocks, per_block)
    expert_ids = jnp.arange(EXPERTS, dtype=jnp.int32)
    onehot = (chosen[:, :, None] == expert_ids[None, None, :]).astype(jnp.int32)
    earlier = jnp.cumsum(onehot, axis=1) - onehot
    position = jnp.sum(earlier * onehot, axis=2)
    token_of = jnp.arange(per_block, dtype=jnp.int32) // TOP
    block_start = (jnp.arange(num_blocks, dtype=jnp.int32) * TOK_DEV)[:, None]
    slot_ids = jnp.arange(CAP, dtype=jnp.int32)

    def one_expert(state, inputs):
        y_total, dx_total = state
        expert_id, wg_e, wu_e, wd_e = inputs
        hits = (chosen == expert_id)[:, None, :] & (position[:, None, :] == slot_ids[None, :, None])
        row_token = (jnp.sum(jnp.where(hits, token_of[None, None, :], 0), axis=2) + block_start)
        row_token = row_token.reshape(num_blocks * CAP).astype(jnp.int32)
        row_gate = jnp.sum(jnp.where(hits, gate_flat[:, None, :], 0.0), axis=2).reshape(num_blocks * CAP)
        x_rows = tokens[row_token]
        gate_val = jnp.dot(x_rows, wg_e, preferred_element_type=jnp.float32)
        up_val = jnp.dot(x_rows, wu_e, preferred_element_type=jnp.float32)
        hidden = (jax.nn.silu(gate_val) * up_val).astype(jnp.bfloat16)
        expert_out = jnp.dot(hidden, wd_e, preferred_element_type=jnp.float32).astype(jnp.bfloat16)
        y_total = y_total.at[row_token].add(row_gate[:, None] * expert_out.astype(jnp.float32))
        scaled = (row_gate[:, None] * grad_out[row_token].astype(jnp.float32)).astype(jnp.bfloat16)
        d_hidden = jnp.dot(scaled, wd_e.T, preferred_element_type=jnp.float32)
        sig_gate = jax.nn.sigmoid(gate_val)
        d_gate = (d_hidden * up_val * sig_gate * (1.0 + gate_val * (1.0 - sig_gate))).astype(jnp.bfloat16)
        d_up = (d_hidden * gate_val * sig_gate).astype(jnp.bfloat16)
        d_rows = (jnp.dot(d_gate, wg_e.T, preferred_element_type=jnp.float32)
                  + jnp.dot(d_up, wu_e.T, preferred_element_type=jnp.float32)).astype(jnp.bfloat16)
        dx_total = dx_total.at[row_token].add(d_rows.astype(jnp.float32))
        grads = (jnp.dot(x_rows.T, d_gate, preferred_element_type=jnp.float32).astype(jnp.bfloat16),
                 jnp.dot(x_rows.T, d_up, preferred_element_type=jnp.float32).astype(jnp.bfloat16),
                 jnp.dot(hidden.T, scaled, preferred_element_type=jnp.float32).astype(jnp.bfloat16))
        return (y_total, dx_total), grads

    start_state = (jnp.zeros((TOKENS, D), jnp.float32), jnp.zeros((TOKENS, D), jnp.float32))
    final_state, grads = lax.scan(one_expert, start_state, (expert_ids, w_gate, w_up, w_down))
    mixed = final_state[0].astype(jnp.bfloat16)
    grad_tokens = final_state[1].astype(jnp.bfloat16)
    return (mixed, grad_tokens, grads[0], grads[1], grads[2])
```

```python
import functools

import jax
import jax.numpy as jnp
from jax import lax
from jax.experimental import pallas as pl
from jax.experimental.pallas import tpu as pltpu
from jax.sharding import PartitionSpec as P

CAP = 32
MESH = pl.DeviceIdType.MESH
F32 = jnp.float32
BF16 = jnp.bfloat16
NN = (((1,), (0,)), ((), ()))
NT = (((1,), (1,)), ((), ()))


def dot(a, b, dims=NN):
    return lax.dot_general(a, b, dims, preferred_element_type=F32)


def chunk_order(dp):
    return {4: (0, 2, 1, 3), 2: (0, 1), 1: (0,)}[dp]


def kernel(
    dp, ex, pipe,
    routes_ref, gates_ref, tok_ref, go_ref, wg_hbm, wu_hbm, wd_hbm,
    mixed_ref, gtok_ref, gg_hbm, gu_hbm, gd_hbm,
    wg, wu, wd, onehot, mixw, onehot_t, mix_hi, mix_lo,
    out_x, out_g, rows_x, rows_g, part, ring_in, ring_out, full,
    acc_g, acc_u, acc_d, grad_g, grad_u, grad_d, eo_buf, dr_buf, ret_e, ret_d,
    w_sem, self_sem, send_a2a, recv_x, recv_g, send_ret, recv_ret,
    ring_send, ring_recv, full_send, full_recv, store_sem,
):
    p = lax.axis_index("pipe")
    y = lax.axis_index("dp")
    e = lax.axis_index("expert")
    me = y * ex + e
    groups = dp * ex
    ff = wg.shape[1]
    width = wg.shape[0]
    rows = ex * CAP
    fw = ff // pipe
    rel = chunk_order(dp)
    nxt = lax.rem(p + 1, pipe)
    prv = lax.rem(p + pipe - 1, pipe)
    half = pipe // 2

    loads = [
        pltpu.make_async_copy(src, dst, w_sem.at[i])
        for i, (src, dst) in enumerate(((wg_hbm, wg), (wu_hbm, wu), (wd_hbm, wd)))
    ]
    for load in loads:
        load.start()

    barrier = pltpu.get_barrier_semaphore()
    for r in range(dp):
        for k in range(ex):
            if r == 0 and k == 0:
                continue
            pl.semaphore_signal(
                barrier, inc=1, device_id_type=MESH,
                device_id={"dp": lax.rem(y + r, dp), "expert": lax.rem(e + k, ex)},
            )
    for other in (prv, nxt):
        pl.semaphore_signal(barrier, inc=1, device_id={"pipe": other}, device_id_type=MESH)

    toks = tok_ref.shape[0]
    eid = lax.broadcasted_iota(jnp.int32, (groups, toks), 0)
    member = jnp.zeros((groups, toks), F32)
    gate_of = jnp.zeros((groups, toks), F32)
    for k in range(routes_ref.shape[0]):
        hit = routes_ref[k : k + 1, :] == eid
        member += jnp.where(hit, 1.0, 0.0)
        gate_of += jnp.where(hit, gates_ref[k : k + 1, :], 0.0)
    before = jnp.where(
        lax.broadcasted_iota(jnp.int32, (toks, toks), 0)
        < lax.broadcasted_iota(jnp.int32, (toks, toks), 1),
        1.0, 0.0,
    ).astype(BF16)
    slot = jnp.where(member > 0.0, dot(member.astype(BF16), before), -1.0)
    slot_id = lax.broadcasted_iota(jnp.int32, (CAP, toks), 0).astype(F32)
    for i in range(groups):
        filled = slot[i : i + 1, :] == slot_id
        onehot[i * CAP : (i + 1) * CAP, :] = jnp.where(filled, 1.0, 0.0)
        mixw[i * CAP : (i + 1) * CAP, :] = jnp.where(filled, gate_of[i : i + 1, :], 0.0)
    tokens = tok_ref[...]
    grad_out = go_ref[...]
    step_rows = 256 if groups * CAP % 256 == 0 else groups * CAP
    for i in range(groups * CAP // step_rows):
        span = slice(i * step_rows, (i + 1) * step_rows)
        block = slice(i * step_rows // CAP, (i + 1) * step_rows // CAP)
        pick = onehot[span, :].astype(BF16)
        gate_row = jnp.sum(mixw[span, :], axis=1, keepdims=True)
        out_x[block] = dot(pick, tokens).astype(BF16).reshape(step_rows // CAP, CAP, width)
        out_g[block] = (
            (gate_row * dot(pick, grad_out)).astype(BF16).reshape(step_rows // CAP, CAP, width)
        )

    pl.semaphore_wait(barrier, groups - 1 + 2)

    own_copies = []
    for c in range(dp):
        to_y = lax.rem(y - rel[c] + dp, dp)
        for src, dst, recv in ((out_x, rows_x, recv_x), (out_g, rows_g, recv_g)):
            for k in range(ex):
                to_e = lax.rem(e + k, ex)
                if rel[c] == 0 and k == 0:
                    copy = pltpu.make_async_copy(
                        src.at[me], dst.at[c, e], self_sem.at[len(own_copies)]
                    )
                    copy.start()
                    own_copies.append(copy)
                    continue
                pltpu.make_async_remote_copy(
                    src_ref=src.at[to_y * ex + to_e],
                    dst_ref=dst.at[c, e],
                    send_sem=send_a2a,
                    recv_sem=recv.at[c],
                    device_id={"dp": to_y, "expert": to_e},
                    device_id_type=MESH,
                ).start()

    onehot_t[...] = onehot[...].T.astype(BF16)
    mix_t = mixw[...].T
    mix_top = mix_t.astype(BF16)
    mix_hi[...] = mix_top
    mix_lo[...] = (mix_t - mix_top.astype(F32)).astype(BF16)

    def bytes_wait(ref, sem):
        pltpu.make_async_copy(ref, ref, sem).wait()

    def arrive(c, buf, recv, own):
        if rel[c] == 0:
            own.wait()
            if ex > 1:
                view = buf.at[c, pl.ds(0, ex - 1)]
                bytes_wait(view, recv.at[c])
        else:
            bytes_wait(buf.at[c], recv.at[c])

    def x_of(c):
        return rows_x[c].reshape(rows, width)

    def g_of(c):
        return rows_g[c].reshape(rows, width)

    tile = 256

    def partial(c, q):
        a = x_of(c) if q < 2 else g_of(c)
        for n in range(ff // tile):
            cols = slice(n * tile, (n + 1) * tile)
            if q == 2:
                res = dot(a, wd[cols, :], NT)
            else:
                res = dot(a, (wg, wu)[q][:, cols])
            for i in range(tile // fw):
                part[c % 2, q, n * (tile // fw) + i] = res[:, i * fw : (i + 1) * fw]

    def hops(c, d):
        return half if (c % 2 == 0) == (d == 0) else half - 1

    def place(c, d, t):
        return t if hops(c, d) == half else half + t

    def ring_step(c, t):
        for q in range(3):
            for d in range(2):
                n = hops(c, d)
                if t >= n:
                    continue
                owner = lax.rem(p - n + t + pipe, pipe) if d == 0 else lax.rem(p + n - t, pipe)
                value = part[c % 2, q, owner]
                if t > 0:
                    got = place(c, d, t - 1)
                    bytes_wait(ring_in.at[c, q, got], ring_recv.at[c, q, got])
                    value = value + ring_in[c, q, got].astype(F32)
                m = place(c, d, t)
                ring_out[c, q, m] = value.astype(BF16)
                pltpu.make_async_remote_copy(
                    src_ref=ring_out.at[c, q, m],
                    dst_ref=ring_in.at[c, q, m],
                    send_sem=ring_send,
                    recv_sem=ring_recv.at[c, q, m],
                    device_id={"pipe": prv if d == 0 else nxt},
                    device_id_type=MESH,
                ).start()

    def spread_start(c, q, d, t):
        owner = lax.rem(p + t, pipe) if d == 0 else lax.rem(p - t + pipe, pipe)
        m = place(c, d, t)
        pltpu.make_async_remote_copy(
            src_ref=full.at[q, c, owner],
            dst_ref=full.at[q, c, owner],
            send_sem=full_send,
            recv_sem=full_recv.at[c, q, m],
            device_id={"pipe": prv if d == 0 else nxt},
            device_id_type=MESH,
        ).start()

    def spread_wait(c, q, d, t):
        m = place(c, d, t)
        owner = lax.rem(p + t + 1, pipe) if d == 0 else lax.rem(p - t - 1 + pipe, pipe)
        bytes_wait(full.at[q, c, owner], full_recv.at[c, q, m])

    def activate(c):
        sums = []
        for q in range(3):
            value = part[c % 2, q, p]
            for d in range(2):
                m = place(c, d, hops(c, d) - 1)
                bytes_wait(ring_in.at[c, q, m], ring_recv.at[c, q, m])
                value = value + ring_in[c, q, m].astype(F32)
            sums.append(value)
            if q == 1:
                gate, up = sums
                sig = jax.nn.sigmoid(gate)
                full[0, c, p] = (gate * sig * up).astype(BF16)
                for d in range(2):
                    spread_start(c, 0, d, 0)
        gate, up, dh = sums
        full[1, c, p] = (dh * up * sig * (1.0 + gate * (1.0 - sig))).astype(BF16)
        for d in range(2):
            spread_start(c, 1, d, 0)
        full[2, c, p] = (dh * gate * sig).astype(BF16)
        for d in range(2):
            spread_start(c, 2, d, 0)

    def spread_step(c, t):
        for q in range(3):
            for d in range(2):
                if t < hops(c, d):
                    spread_wait(c, q, d, t - 1)
                    spread_start(c, q, d, t)

    def spread_end(c, q):
        for d in range(2):
            spread_wait(c, q, d, hops(c, d) - 1)

    def joined(q, c):
        return jnp.concatenate([full[q, c, i] for i in range(pipe)], axis=1)

    def send_back(c, buf, ret, i):
        to_y = lax.rem(y + rel[c], dp)
        for k in range(ex):
            to_e = lax.rem(e + k, ex)
            if rel[c] == 0 and k == 0:
                copy = pltpu.make_async_copy(buf.at[c, e], ret.at[me], self_sem.at[2 + i])
                copy.start()
                own_copies.append(copy)
                continue
            pltpu.make_async_remote_copy(
                src_ref=buf.at[c, to_e],
                dst_ref=ret.at[me],
                send_sem=send_ret,
                recv_sem=recv_ret.at[i],
                device_id={"dp": to_y, "expert": to_e},
                device_id_type=MESH,
            ).start()

    wtile = 256 if width % 256 == 0 else width

    def expert_out(c):
        h = joined(0, c)
        for n in range(width // wtile):
            cols = slice(n * wtile, (n + 1) * wtile)
            eo_buf[c, :, :, cols] = dot(h, wd[:, cols]).astype(BF16).reshape(ex, CAP, wtile)
        send_back(c, eo_buf, ret_e, 0)

    def input_grad(c):
        dg = joined(1, c)
        du = joined(2, c)
        for n in range(width // wtile):
            cols = slice(n * wtile, (n + 1) * wtile)
            res = dot(dg, wg[cols, :], NT) + dot(du, wu[cols, :], NT)
            dr_buf[c, :, :, cols] = res.astype(BF16).reshape(ex, CAP, wtile)
        send_back(c, dr_buf, ret_d, 1)

    stores = []

    def keep(acc, out, index, c, res):
        if c > 0:
            res = res + acc[index]
        if c == dp - 1:
            out[index] = res.astype(BF16)
        else:
            acc[index] = res

    def gate_grads(c):
        xt = x_of(c).T
        for q, acc, out in ((1, acc_g, grad_g), (2, acc_u, grad_u)):
            for n in range(ff // tile):
                per = tile // fw
                b = jnp.concatenate([full[q, c, n * per + i] for i in range(per)], axis=1)
                keep(acc, out, (slice(None), slice(n * tile, (n + 1) * tile)), c, dot(xt, b))

    def down_grad(c):
        g = g_of(c)
        for i in range(pipe):
            ht = full[0, c, i].T
            keep(acc_d, grad_d, (slice(i * fw, (i + 1) * fw), slice(None)), c, dot(ht, g))

    arrive(0, rows_x, recv_x, own_copies[0])
    loads[0].wait()
    loads[1].wait()
    partial(0, 0)
    partial(0, 1)
    arrive(0, rows_g, recv_g, own_copies[1])
    loads[2].wait()
    partial(0, 2)
    for period in range(dp + 1):
        for t in range(half):
            if period < dp:
                ring_step(period, t)
            if period >= 1:
                if t == 0:
                    activate(period - 1)
                else:
                    spread_step(period - 1, t)
            if t == 0 and period >= 2:
                for q in range(3):
                    spread_end(period - 2, q)
            if period + 1 < dp:
                if t == 0:
                    arrive(period + 1, rows_x, recv_x, None)
                    partial(period + 1, 0)
                elif t == 1:
                    partial(period + 1, 1)
                elif t == 2:
                    arrive(period + 1, rows_g, recv_g, None)
                    partial(period + 1, 2)
            if period >= 2:
                if t == 0:
                    expert_out(period - 2)
                elif t == 1:
                    input_grad(period - 2)
                elif t == 2:
                    gate_grads(period - 2)
                else:
                    down_grad(period - 2)
    last = dp - 1
    spread_end(last, 0)
    expert_out(last)
    spread_end(last, 1)
    spread_end(last, 2)
    input_grad(last)
    gate_grads(last)
    down_grad(last)
    for i, (src, dst) in enumerate(((grad_g, gg_hbm), (grad_u, gu_hbm), (grad_d, gd_hbm))):
        copy = pltpu.make_async_copy(src, dst, store_sem.at[i])
        copy.start()
        stores.append(copy)

    own_copies[2].wait()
    bytes_wait(ret_e.at[pl.ds(0, groups - 1)], recv_ret.at[0])
    back = ret_e[...].reshape(groups * CAP, width)
    mixed_ref[...] = (dot(mix_hi[...], back) + dot(mix_lo[...], back)).astype(BF16)
    own_copies[3].wait()
    bytes_wait(ret_d.at[pl.ds(0, groups - 1)], recv_ret.at[1])
    back = ret_d[...].reshape(groups * CAP, width)
    gtok_ref[...] = dot(onehot_t[...], back).astype(BF16)

    for _ in range(2):
        bytes_wait(out_x.at[pl.ds(0, groups - 1)], send_a2a)
        bytes_wait(out_x.at[pl.ds(0, groups - 1)], send_ret)
    bytes_wait(ring_out, ring_send)
    bytes_wait(ring_out, full_send)
    for copy in stores:
        copy.wait()


def local(sizes, tokens, routes, gates, w_gate, w_up, w_down, grad_out):
    dp, ex, pipe = sizes
    toks, width = tokens.shape
    ff = w_gate.shape[2]
    groups, rows, fw = dp * ex, ex * CAP, ff // pipe
    vmem = pl.BlockSpec(memory_space=pltpu.VMEM)
    hbm = pl.BlockSpec(memory_space=pl.ANY)
    dma = pltpu.SemaphoreType.DMA
    messages = pipe - 1
    mixed, grad_tokens, grad_gate, grad_up, grad_down = pl.pallas_call(
        functools.partial(kernel, dp, ex, pipe),
        out_shape=(
            jax.ShapeDtypeStruct((toks, width), BF16),
            jax.ShapeDtypeStruct((toks, width), BF16),
            jax.ShapeDtypeStruct((width, ff), BF16),
            jax.ShapeDtypeStruct((width, ff), BF16),
            jax.ShapeDtypeStruct((ff, width), BF16),
        ),
        in_specs=[vmem, vmem, vmem, vmem, hbm, hbm, hbm],
        out_specs=(vmem, vmem, hbm, hbm, hbm),
        scratch_shapes=[
            pltpu.VMEM((width, ff), BF16),
            pltpu.VMEM((width, ff), BF16),
            pltpu.VMEM((ff, width), BF16),
            pltpu.VMEM((groups * CAP, toks), F32),
            pltpu.VMEM((groups * CAP, toks), F32),
            pltpu.VMEM((toks, groups * CAP), BF16),
            pltpu.VMEM((toks, groups * CAP), BF16),
            pltpu.VMEM((toks, groups * CAP), BF16),
            pltpu.VMEM((groups, CAP, width), BF16),
            pltpu.VMEM((groups, CAP, width), BF16),
            pltpu.VMEM((dp, ex, CAP, width), BF16),
            pltpu.VMEM((dp, ex, CAP, width), BF16),
            pltpu.VMEM((2, 3, pipe, rows, fw), F32),
            pltpu.VMEM((dp, 3, messages, rows, fw), BF16),
            pltpu.VMEM((dp, 3, messages, rows, fw), BF16),
            pltpu.VMEM((3, dp, pipe, rows, fw), BF16),
            pltpu.VMEM((width, ff), F32),
            pltpu.VMEM((width, ff), F32),
            pltpu.VMEM((ff, width), F32),
            pltpu.VMEM((width, ff), BF16),
            pltpu.VMEM((width, ff), BF16),
            pltpu.VMEM((ff, width), BF16),
            pltpu.VMEM((dp, ex, CAP, width), BF16),
            pltpu.VMEM((dp, ex, CAP, width), BF16),
            pltpu.VMEM((groups, CAP, width), BF16),
            pltpu.VMEM((groups, CAP, width), BF16),
            dma((3,)),
            dma((4,)),
            dma,
            dma((dp,)),
            dma((dp,)),
            dma,
            dma((2,)),
            dma,
            dma((dp, 3, messages)),
            dma,
            dma((dp, 3, messages)),
            dma((3,)),
        ],
        compiler_params=pltpu.CompilerParams(
            collective_id=0, has_side_effects=True, vmem_limit_bytes=60 * 1024 * 1024
        ),
    )(
        routes.T, gates.T, tokens, grad_out,
        w_gate.reshape(width, ff), w_up.reshape(width, ff), w_down.reshape(ff, width),
    )
    return (
        mixed,
        grad_tokens,
        grad_gate.reshape(1, width, ff),
        grad_up.reshape(1, width, ff),
        grad_down.reshape(1, ff, width),
    )


def solution(mesh):
    both = ("dp", "expert")
    sizes = (mesh.shape["dp"], mesh.shape["expert"], mesh.shape["pipe"])
    return jax.shard_map(
        functools.partial(local, sizes),
        mesh=mesh,
        in_specs=(
            P(both, "pipe"),
            P(both, None),
            P(both, None),
            P(both, "pipe", None),
            P(both, "pipe", None),
            P(both, None, "pipe"),
            P(both, "pipe"),
        ),
        out_specs=(
            P(both, "pipe"),
            P(both, "pipe"),
            P(both, "pipe", None),
            P(both, "pipe", None),
            P(both, None, "pipe"),
        ),
        check_vma=False,
    )
```

```python
import functools

import jax
import jax.numpy as jnp
from jax import lax
from jax.experimental import pallas as pl
from jax.experimental.pallas import tpu as pltpu
from jax.sharding import PartitionSpec as P

CAP = 32
MESH = pl.DeviceIdType.MESH
F32 = jnp.float32
BF16 = jnp.bfloat16
NN = (((1,), (0,)), ((), ()))
NT = (((1,), (1,)), ((), ()))


def dot(a, b, dims=NN):
    return lax.dot_general(a, b, dims, preferred_element_type=F32)


def chunk_order(dp):
    return {4: (0, 1, 2, 3), 2: (0, 1), 1: (0,)}[dp]


def kernel(
    dp, ex, pipe,
    routes_ref, gates_ref, tok_ref, go_ref, wg_hbm, wu_hbm, wd_hbm,
    mixed_ref, gtok_ref, gg_hbm, gu_hbm, gd_hbm,
    wg, wu, wd, onehot, mixw, onehot_t, mix_hi, mix_lo,
    out_x, out_g, rows_x, rows_g, part, ring_in, ring_out, full,
    acc_g, acc_u, acc_d, grad_g, grad_u, grad_d, eo_buf, dr_buf, ret_e, ret_d,
    w_sem, self_sem, send_a2a, recv_x, recv_g, send_ret, recv_ret,
    ring_send, ring_recv, full_send, full_recv, store_sem,
):
    p = lax.axis_index("pipe")
    y = lax.axis_index("dp")
    e = lax.axis_index("expert")
    me = y * ex + e
    groups = dp * ex
    ff = wg.shape[1]
    width = wg.shape[0]
    rows = ex * CAP
    fw = ff // pipe
    rel = chunk_order(dp)
    nxt = lax.rem(p + 1, pipe)
    prv = lax.rem(p + pipe - 1, pipe)
    half = pipe // 2

    loads = [
        pltpu.make_async_copy(src, dst, w_sem.at[i])
        for i, (src, dst) in enumerate(((wg_hbm, wg), (wu_hbm, wu), (wd_hbm, wd)))
    ]
    for load in loads:
        load.start()

    barrier = pltpu.get_barrier_semaphore()
    for r in range(dp):
        for k in range(ex):
            if r == 0 and k == 0:
                continue
            pl.semaphore_signal(
                barrier, inc=1, device_id_type=MESH,
                device_id={"dp": lax.rem(y + r, dp), "expert": lax.rem(e + k, ex)},
            )
    for other in (prv, nxt):
        pl.semaphore_signal(barrier, inc=1, device_id={"pipe": other}, device_id_type=MESH)

    toks = tok_ref.shape[0]
    eid = lax.broadcasted_iota(jnp.int32, (groups, toks), 0)
    member = jnp.zeros((groups, toks), F32)
    gate_of = jnp.zeros((groups, toks), F32)
    for k in range(routes_ref.shape[0]):
        hit = routes_ref[k : k + 1, :] == eid
        member += jnp.where(hit, 1.0, 0.0)
        gate_of += jnp.where(hit, gates_ref[k : k + 1, :], 0.0)
    before = jnp.where(
        lax.broadcasted_iota(jnp.int32, (toks, toks), 0)
        < lax.broadcasted_iota(jnp.int32, (toks, toks), 1),
        1.0, 0.0,
    ).astype(BF16)
    slot = jnp.where(member > 0.0, dot(member.astype(BF16), before), -1.0)
    slot_id = lax.broadcasted_iota(jnp.int32, (CAP, toks), 0).astype(F32)
    for i in range(groups):
        filled = slot[i : i + 1, :] == slot_id
        onehot[i * CAP : (i + 1) * CAP, :] = jnp.where(filled, 1.0, 0.0)
        mixw[i * CAP : (i + 1) * CAP, :] = jnp.where(filled, gate_of[i : i + 1, :], 0.0)
    tokens = tok_ref[...]
    grad_out = go_ref[...]
    step_rows = 256 if groups * CAP % 256 == 0 else groups * CAP
    for i in range(groups * CAP // step_rows):
        span = slice(i * step_rows, (i + 1) * step_rows)
        block = slice(i * step_rows // CAP, (i + 1) * step_rows // CAP)
        pick = onehot[span, :].astype(BF16)
        gate_row = jnp.sum(mixw[span, :], axis=1, keepdims=True)
        out_x[block] = dot(pick, tokens).astype(BF16).reshape(step_rows // CAP, CAP, width)
        out_g[block] = (
            (gate_row * dot(pick, grad_out)).astype(BF16).reshape(step_rows // CAP, CAP, width)
        )

    pl.semaphore_wait(barrier, groups - 1 + 2)

    own_copies = []

    def dispatch(c):
        to_y = lax.rem(y - rel[c] + dp, dp)
        for src, dst, recv in ((out_x, rows_x, recv_x), (out_g, rows_g, recv_g)):
            for k in range(ex):
                to_e = lax.rem(e + k, ex)
                if rel[c] == 0 and k == 0:
                    copy = pltpu.make_async_copy(
                        src.at[me], dst.at[c, e], self_sem.at[len(own_copies)]
                    )
                    copy.start()
                    own_copies.append(copy)
                    continue
                pltpu.make_async_remote_copy(
                    src_ref=src.at[to_y * ex + to_e],
                    dst_ref=dst.at[c, e],
                    send_sem=send_a2a,
                    recv_sem=recv.at[c],
                    device_id={"dp": to_y, "expert": to_e},
                    device_id_type=MESH,
                ).start()

    for c in range(min(dp, 2)):
        dispatch(c)

    onehot_t[...] = onehot[...].T.astype(BF16)
    mix_t = mixw[...].T
    mix_top = mix_t.astype(BF16)
    mix_hi[...] = mix_top
    mix_lo[...] = (mix_t - mix_top.astype(F32)).astype(BF16)

    def bytes_wait(ref, sem):
        pltpu.make_async_copy(ref, ref, sem).wait()

    def arrive(c, buf, recv, own):
        if rel[c] == 0:
            own.wait()
            if ex > 1:
                view = buf.at[c, pl.ds(0, ex - 1)]
                bytes_wait(view, recv.at[c])
        else:
            bytes_wait(buf.at[c], recv.at[c])

    def x_of(c):
        return rows_x[c].reshape(rows, width)

    def g_of(c):
        return rows_g[c].reshape(rows, width)

    tile = 256

    def partial(c, q):
        a = x_of(c) if q < 2 else g_of(c)
        for n in range(ff // tile):
            cols = slice(n * tile, (n + 1) * tile)
            if q == 2:
                res = dot(a, wd[cols, :], NT)
            else:
                res = dot(a, (wg, wu)[q][:, cols])
            for i in range(tile // fw):
                part[c % 2, q, n * (tile // fw) + i] = res[:, i * fw : (i + 1) * fw]

    def hops(c, d):
        return half if (c % 2 == 0) == (d == 0) else half - 1

    def place(c, d, t):
        return t if hops(c, d) == half else half + t

    def ring_step(c, t):
        for q in range(3):
            for d in range(2):
                n = hops(c, d)
                if t >= n:
                    continue
                owner = lax.rem(p - n + t + pipe, pipe) if d == 0 else lax.rem(p + n - t, pipe)
                value = part[c % 2, q, owner]
                if t > 0:
                    got = place(c, d, t - 1)
                    bytes_wait(ring_in.at[c, q, got], ring_recv.at[c, q, got])
                    value = value + ring_in[c, q, got].astype(F32)
                m = place(c, d, t)
                ring_out[c, q, m] = value.astype(BF16)
                pltpu.make_async_remote_copy(
                    src_ref=ring_out.at[c, q, m],
                    dst_ref=ring_in.at[c, q, m],
                    send_sem=ring_send,
                    recv_sem=ring_recv.at[c, q, m],
                    device_id={"pipe": prv if d == 0 else nxt},
                    device_id_type=MESH,
                ).start()

    def spread_start(c, q, d, t):
        owner = lax.rem(p + t, pipe) if d == 0 else lax.rem(p - t + pipe, pipe)
        m = place(c, d, t)
        pltpu.make_async_remote_copy(
            src_ref=full.at[q, c, owner],
            dst_ref=full.at[q, c, owner],
            send_sem=full_send,
            recv_sem=full_recv.at[c, q, m],
            device_id={"pipe": prv if d == 0 else nxt},
            device_id_type=MESH,
        ).start()

    def spread_wait(c, q, d, t):
        m = place(c, d, t)
        owner = lax.rem(p + t + 1, pipe) if d == 0 else lax.rem(p - t - 1 + pipe, pipe)
        bytes_wait(full.at[q, c, owner], full_recv.at[c, q, m])

    def activate(c):
        sums = []
        for q in range(3):
            value = part[c % 2, q, p]
            for d in range(2):
                m = place(c, d, hops(c, d) - 1)
                bytes_wait(ring_in.at[c, q, m], ring_recv.at[c, q, m])
                value = value + ring_in[c, q, m].astype(F32)
            sums.append(value)
            if q == 1:
                gate, up = sums
                sig = jax.nn.sigmoid(gate)
                full[0, c, p] = (gate * sig * up).astype(BF16)
                for d in range(2):
                    spread_start(c, 0, d, 0)
        gate, up, dh = sums
        full[1, c, p] = (dh * up * sig * (1.0 + gate * (1.0 - sig))).astype(BF16)
        for d in range(2):
            spread_start(c, 1, d, 0)
        full[2, c, p] = (dh * gate * sig).astype(BF16)
        for d in range(2):
            spread_start(c, 2, d, 0)

    def spread_step(c, t):
        for q in range(3):
            for d in range(2):
                if t < hops(c, d):
                    spread_wait(c, q, d, t - 1)
                    spread_start(c, q, d, t)

    def spread_end(c, q):
        for d in range(2):
            spread_wait(c, q, d, hops(c, d) - 1)

    def joined(q, c):
        return jnp.concatenate([full[q, c, i] for i in range(pipe)], axis=1)

    def send_back(c, buf, ret, i):
        to_y = lax.rem(y + rel[c], dp)
        for k in range(ex):
            to_e = lax.rem(e + k, ex)
            if rel[c] == 0 and k == 0:
                copy = pltpu.make_async_copy(buf.at[c, e], ret.at[me], self_sem.at[2 + i])
                copy.start()
                own_copies.append(copy)
                continue
            pltpu.make_async_remote_copy(
                src_ref=buf.at[c, to_e],
                dst_ref=ret.at[me],
                send_sem=send_ret,
                recv_sem=recv_ret.at[i],
                device_id={"dp": to_y, "expert": to_e},
                device_id_type=MESH,
            ).start()

    wtile = 256 if width % 256 == 0 else width

    def expert_out(c):
        h = joined(0, c)
        for n in range(width // wtile):
            cols = slice(n * wtile, (n + 1) * wtile)
            eo_buf[c, :, :, cols] = dot(h, wd[:, cols]).astype(BF16).reshape(ex, CAP, wtile)
        send_back(c, eo_buf, ret_e, 0)

    def input_grad(c):
        dg = joined(1, c)
        du = joined(2, c)
        for n in range(width // wtile):
            cols = slice(n * wtile, (n + 1) * wtile)
            res = dot(dg, wg[cols, :], NT) + dot(du, wu[cols, :], NT)
            dr_buf[c, :, :, cols] = res.astype(BF16).reshape(ex, CAP, wtile)
        send_back(c, dr_buf, ret_d, 1)

    stores = []

    def keep(acc, out, index, c, res):
        if c > 0:
            res = res + acc[index]
        if c == dp - 1:
            out[index] = res.astype(BF16)
        else:
            acc[index] = res

    def gate_grads(c):
        xt = x_of(c).T
        for q, acc, out in ((1, acc_g, grad_g), (2, acc_u, grad_u)):
            for n in range(ff // tile):
                per = tile // fw
                b = jnp.concatenate([full[q, c, n * per + i] for i in range(per)], axis=1)
                keep(acc, out, (slice(None), slice(n * tile, (n + 1) * tile)), c, dot(xt, b))

    def down_grad(c):
        g = g_of(c)
        for i in range(pipe):
            ht = full[0, c, i].T
            keep(acc_d, grad_d, (slice(i * fw, (i + 1) * fw), slice(None)), c, dot(ht, g))

    arrive(0, rows_x, recv_x, own_copies[0])
    loads[0].wait()
    loads[1].wait()
    partial(0, 0)
    partial(0, 1)
    arrive(0, rows_g, recv_g, own_copies[1])
    loads[2].wait()
    partial(0, 2)
    for period in range(dp + 1):
        for t in range(half):
            if period < dp:
                ring_step(period, t)
            if period == 0 and t == 0:
                for c in range(2, dp):
                    dispatch(c)
            if period >= 1:
                if t == 0:
                    activate(period - 1)
                else:
                    spread_step(period - 1, t)
            if t == 0 and period >= 2:
                for q in range(3):
                    spread_end(period - 2, q)
            if period + 1 < dp:
                first = 1 if period == 0 else 0
                if t == first:
                    arrive(period + 1, rows_x, recv_x, None)
                    partial(period + 1, 0)
                elif t == first + 1:
                    partial(period + 1, 1)
                elif t == first + 2:
                    arrive(period + 1, rows_g, recv_g, None)
                    partial(period + 1, 2)
            if period >= 2:
                if t == 0:
                    expert_out(period - 2)
                elif t == 1:
                    input_grad(period - 2)
                elif t == 2:
                    gate_grads(period - 2)
                else:
                    down_grad(period - 2)
    last = dp - 1
    spread_end(last, 0)
    expert_out(last)
    down_grad(last)

    def store(i, src, dst):
        copy = pltpu.make_async_copy(src, dst, store_sem.at[i])
        copy.start()
        stores.append(copy)

    store(2, grad_d, gd_hbm)
    spread_end(last, 1)
    spread_end(last, 2)
    input_grad(last)
    gate_grads(last)
    store(0, grad_g, gg_hbm)
    store(1, grad_u, gu_hbm)

    own_copies[2].wait()
    bytes_wait(ret_e.at[pl.ds(0, groups - 1)], recv_ret.at[0])
    back = ret_e[...].reshape(groups * CAP, width)
    mixed_ref[...] = (dot(mix_hi[...], back) + dot(mix_lo[...], back)).astype(BF16)
    own_copies[3].wait()
    bytes_wait(ret_d.at[pl.ds(0, groups - 1)], recv_ret.at[1])
    back = ret_d[...].reshape(groups * CAP, width)
    gtok_ref[...] = dot(onehot_t[...], back).astype(BF16)

    for _ in range(2):
        bytes_wait(out_x.at[pl.ds(0, groups - 1)], send_a2a)
        bytes_wait(out_x.at[pl.ds(0, groups - 1)], send_ret)
    bytes_wait(ring_out, ring_send)
    bytes_wait(ring_out, full_send)
    for copy in stores:
        copy.wait()


def hand_out(count, *refs):
    src, dst, buf = (refs[i * count : (i + 1) * count] for i in range(3))
    in_sem, out_sem = refs[3 * count :]
    ins = [pltpu.make_async_copy(src[i], buf[i], in_sem.at[i]) for i in range(count)]
    outs = [pltpu.make_async_copy(buf[i], dst[i], out_sem.at[i]) for i in range(count)]
    for copy in ins:
        copy.start()
    for i in range(count):
        ins[i].wait()
        outs[i].start()
    for copy in outs:
        copy.wait()


def local(sizes, tokens, routes, gates, w_gate, w_up, w_down, grad_out):
    dp, ex, pipe = sizes
    toks, width = tokens.shape
    ff = w_gate.shape[2]
    groups, rows, fw = dp * ex, ex * CAP, ff // pipe
    vmem = pl.BlockSpec(memory_space=pltpu.VMEM)
    hbm = pl.BlockSpec(memory_space=pl.ANY)
    dma = pltpu.SemaphoreType.DMA
    messages = pipe - 1
    results = pl.pallas_call(
        functools.partial(kernel, dp, ex, pipe),
        out_shape=(
            jax.ShapeDtypeStruct((toks, width), BF16),
            jax.ShapeDtypeStruct((toks, width), BF16),
            jax.ShapeDtypeStruct((width, ff), BF16),
            jax.ShapeDtypeStruct((width, ff), BF16),
            jax.ShapeDtypeStruct((ff, width), BF16),
        ),
        in_specs=[vmem, vmem, vmem, vmem, hbm, hbm, hbm],
        out_specs=(vmem, vmem, hbm, hbm, hbm),
        scratch_shapes=[
            pltpu.VMEM((width, ff), BF16),
            pltpu.VMEM((width, ff), BF16),
            pltpu.VMEM((ff, width), BF16),
            pltpu.VMEM((groups * CAP, toks), F32),
            pltpu.VMEM((groups * CAP, toks), F32),
            pltpu.VMEM((toks, groups * CAP), BF16),
            pltpu.VMEM((toks, groups * CAP), BF16),
            pltpu.VMEM((toks, groups * CAP), BF16),
            pltpu.VMEM((groups, CAP, width), BF16),
            pltpu.VMEM((groups, CAP, width), BF16),
            pltpu.VMEM((dp, ex, CAP, width), BF16),
            pltpu.VMEM((dp, ex, CAP, width), BF16),
            pltpu.VMEM((2, 3, pipe, rows, fw), F32),
            pltpu.VMEM((dp, 3, messages, rows, fw), BF16),
            pltpu.VMEM((dp, 3, messages, rows, fw), BF16),
            pltpu.VMEM((3, dp, pipe, rows, fw), BF16),
            pltpu.VMEM((width, ff), F32),
            pltpu.VMEM((width, ff), F32),
            pltpu.VMEM((ff, width), F32),
            pltpu.VMEM((width, ff), BF16),
            pltpu.VMEM((width, ff), BF16),
            pltpu.VMEM((ff, width), BF16),
            pltpu.VMEM((dp, ex, CAP, width), BF16),
            pltpu.VMEM((dp, ex, CAP, width), BF16),
            pltpu.VMEM((groups, CAP, width), BF16),
            pltpu.VMEM((groups, CAP, width), BF16),
            dma((3,)),
            dma((4,)),
            dma,
            dma((dp,)),
            dma((dp,)),
            dma,
            dma((2,)),
            dma,
            dma((dp, 3, messages)),
            dma,
            dma((dp, 3, messages)),
            dma((3,)),
        ],
        compiler_params=pltpu.CompilerParams(
            collective_id=0, has_side_effects=True, vmem_limit_bytes=60 * 1024 * 1024
        ),
    )(
        routes.T, gates.T, tokens, grad_out,
        w_gate.reshape(width, ff), w_up.reshape(width, ff), w_down.reshape(ff, width),
    )
    count = len(results)
    mixed, grad_tokens, grad_gate, grad_up, grad_down = pl.pallas_call(
        functools.partial(hand_out, count),
        out_shape=tuple(jax.ShapeDtypeStruct(r.shape, r.dtype) for r in results),
        in_specs=[hbm] * count,
        out_specs=(hbm,) * count,
        scratch_shapes=[pltpu.VMEM(r.shape, r.dtype) for r in results] + [dma((count,))] * 2,
        compiler_params=pltpu.CompilerParams(vmem_limit_bytes=60 * 1024 * 1024),
    )(*results)
    return (
        mixed,
        grad_tokens,
        grad_gate.reshape(1, width, ff),
        grad_up.reshape(1, width, ff),
        grad_down.reshape(1, ff, width),
    )


def solution(mesh):
    both = ("dp", "expert")
    sizes = (mesh.shape["dp"], mesh.shape["expert"], mesh.shape["pipe"])
    return jax.shard_map(
        functools.partial(local, sizes),
        mesh=mesh,
        in_specs=(
            P(both, "pipe"),
            P(both, None),
            P(both, None),
            P(both, "pipe", None),
            P(both, "pipe", None),
            P(both, None, "pipe"),
            P(both, "pipe"),
        ),
        out_specs=(
            P(both, "pipe"),
            P(both, "pipe"),
            P(both, "pipe", None),
            P(both, "pipe", None),
            P(both, None, "pipe"),
        ),
        check_vma=False,
    )
```
